32 devices in a mesh: section: 2 (over x), dp: 2 (over y), seq: 4 (over z), mp: 2 (over core).
Axes of the slice: x: 2, y: 2, z: 4, core: 2. Of those that a mesh axis runs over, the one named last changes fastest.
Arguments:
- tokens: bfloat16 [4, 2, 512, 1024], P(None, 'dp', 'seq'), may hold values from -6 to 6
- starts: int32 [4, 2, 512], P(None, 'dp', 'seq'), may hold values 0 or 1
- cotangent: float32 [4, 2, 512, 1024], P(None, 'dp', 'seq'), may hold values from -6 to 6
- gain_one: float32 [2, 1024], P('section'), may hold values from 0.5 to 1.5
- w_in: bfloat16 [2, 3, 1024, 1024], P('section', None, None, 'mp'), may hold values from -0.1875 to 0.1875
- conv_w: float32 [2, 3, 1024], P('section', None, 'mp'), may hold values from -3.5 to 3.5
- w_out: bfloat16 [2, 1024, 1024], P('section', None, 'mp'), may hold values from -0.1875 to 0.1875
- gain_two: float32 [2, 1024], P('section'), may hold values from 0.5 to 1.5
- w_gate: bfloat16 [2, 1024, 4608], P('section', None, 'mp'), may hold values from -0.1875 to 0.1875
- w_up: bfloat16 [2, 1024, 4608], P('section', None, 'mp'), may hold values from -0.1875 to 0.1875
- w_down: bfloat16 [2, 1024, 4608], P('section', None, 'mp'), may hold values from -0.09375 to 0.09375
Outputs:
- ends: float32 [2, 4, 2, 512, 1024], P('section', None, 'dp', 'seq')
- grad_gain_one: float32 [2, 1024], P('section', ('dp', 'seq'))
- grad_w_in: float32 [2, 3, 1024, 1024], P('section', None, ('dp', 'seq'), 'mp')
- grad_conv_w: float32 [2, 3, 2, 512], P('section', None, 'mp', ('dp', 'seq'))
- grad_w_out: float32 [2, 1024, 1024], P('section', ('dp', 'seq'), 'mp')
- grad_gain_two: float32 [2, 1024], P('section', ('dp', 'seq'))
- grad_w_gate: float32 [2, 1024, 4608], P('section', ('dp', 'seq'), 'mp')
- grad_w_up: float32 [2, 1024, 4608], P('section', ('dp', 'seq'), 'mp')
- grad_w_down: float32 [2, 1024, 4608], P('section', ('dp', 'seq'), 'mp')
The draws below stay inside these ranges and needn't reach their ends.
Inputs may be any that keep to these rules, and one draw needn't show every extreme that they name: `starts`: 1 marks the first token of a document; the first token of each sequence begins one whether marked or not.
All inputs are finite; a program needn't handle non-finite values. No bound on the sum of `starts` on one device may be relied on, other than what follows from the above.
Results may differ from the reference program's by a relative error of at most 0.02.
Values may be sent and summed in bfloat16 or wider, within the bound.
No kernel may reach another device: no remote copies, remote signals or barrier semaphores. Data moves between devices by JAX's collectives and lax.ppermute only.
A program may use at most 256 MiB of HBM per device.

```python
import jax
import jax.numpy as jnp
from jax import lax

D = 1024
FF = 4608
KW = 3
MICRO = 4
BATCH = 2
SEQLEN = 512
N_SECTION = 2
N_MP = 2


def place_ends(values, rng, smallest, largest):
    index_at = [jax.random.randint(jax.random.fold_in(rng, axis), (), 0, length) for axis, length in enumerate(values.shape)]
    longest = values.shape.index(max(values.shape))
    neighbour = index_at[:longest] + [(index_at[longest] + 1) % values.shape[longest]] + index_at[longest + 1:]
    return values.at[tuple(index_at)].set(smallest).at[tuple(neighbour)].set(largest)


def level_of(rng, shape, pieces, least, top_value):
    def one(position, shards_of):
        draws = jax.random.uniform(jax.random.fold_in(jax.random.fold_in(rng, 6), position), (shards_of,), jnp.float32, least / len(pieces), top_value / len(pieces))
        return jnp.repeat(jnp.exp(draws), shape[position] // shards_of).reshape((-1,) + (1,) * (len(shape) - position - 1))

    gain = one(*pieces[0])
    for cut in pieces[1:]:
        gain = gain * one(*cut)
    return gain


def gaussian(own_key, shape, width, bound, split=(), kind=jnp.bfloat16):
    values = width * jax.random.normal(own_key, shape, jnp.float32)
    if split:
        values = values * level_of(own_key, shape, split, -0.22, 0.18)
    return jnp.clip(values, -bound, bound).astype(kind)


def setup_inputs(seed: int = 0) -> dict:
    arg_keys = jax.random.split(jax.random.key(seed), 12)
    tokens = gaussian(arg_keys[0], (MICRO, BATCH, SEQLEN, D), 1.0, 6.0, ((1, 2), (2, 4)))
    starts = place_ends((jax.random.randint(arg_keys[1], (MICRO, BATCH, SEQLEN), 0, 48) < 1).astype(jnp.int32), jax.random.fold_in(arg_keys[1], 1), 0, 1)
    cotangent = gaussian(arg_keys[2], (MICRO, BATCH, SEQLEN, D), 1.0, 6.0, ((1, 2), (2, 4)), jnp.float32)
    gain_one = jnp.clip(1.0 + 0.1 * jax.random.normal(arg_keys[3], (N_SECTION, D), jnp.float32), 0.5, 1.5)
    w_in = gaussian(arg_keys[4], (N_SECTION, 3, D, D), D ** -0.5, 0.1875, ((0, 2), (3, 2)))
    conv_w = gaussian(arg_keys[5], (N_SECTION, KW, D), KW ** -0.5, 3.5, ((0, 2), (2, 2)), jnp.float32)
    w_out = gaussian(arg_keys[6], (N_SECTION, D, D), D ** -0.5, 0.1875, ((0, 2), (2, 2)))
    gain_two = jnp.clip(1.0 + 0.1 * jax.random.normal(arg_keys[7], (N_SECTION, D), jnp.float32), 0.5, 1.5)
    w_gate = gaussian(arg_keys[8], (N_SECTION, D, FF), D ** -0.5, 0.1875, ((0, 2), (2, 2)))
    w_up = gaussian(arg_keys[9], (N_SECTION, D, FF), D ** -0.5, 0.1875, ((0, 2), (2, 2)))
    w_down = gaussian(arg_keys[10], (N_SECTION, D, FF), FF ** -0.5, 0.09375, ((0, 2), (2, 2)))
    return dict(tokens=tokens, starts=starts, cotangent=cotangent, gain_one=gain_one, w_in=w_in, conv_w=conv_w, w_out=w_out, gain_two=gain_two, w_gate=w_gate, w_up=w_up, w_down=w_down)


NORM_EPS = 1e-05

def matmul(lhs_mat, rhs_mat):
    return jnp.dot(lhs_mat, rhs_mat, preferred_element_type=jnp.float32)

def norm_forward(hidden, norm_gain):
    inv_rms = lax.rsqrt(lax.optimization_barrier(jnp.mean(hidden * hidden, axis=-1, keepdims=True)) + NORM_EPS)
    return ((hidden * inv_rms * norm_gain).astype(jnp.bfloat16), inv_rms)

def norm_backward(hidden, inv_rms, norm_gain, grad_norm):
    normed = hidden * inv_rms
    scaled = grad_norm * norm_gain
    grad_gain = lax.optimization_barrier(jnp.sum(grad_norm * normed, axis=0))
    grad_hidden = inv_rms * (scaled - normed * lax.optimization_barrier(jnp.mean(scaled * normed, axis=-1, keepdims=True)))
    return (grad_hidden, grad_gain)

def conv_masks(keep_mask):
    before = jnp.concatenate([jnp.ones_like(keep_mask[:, :1]), keep_mask[:, :-1]], axis=1)
    return (keep_mask[:, :, None], (before * keep_mask)[:, :, None])

def layer_forward(hidden, keep_mask, params):
    gain_one, w_in, conv_w, w_out, gain_two, w_gate, w_up, w_down = params
    seq_count, seq_len, feature_dim = hidden.shape
    flat_rows = hidden.reshape(seq_count * seq_len, feature_dim)
    normed_one, inv_one = norm_forward(flat_rows, gain_one)
    b_gate = matmul(normed_one, w_in[0])
    c_gate = matmul(normed_one, w_in[1])
    inner_proj = matmul(normed_one, w_in[2])
    gated_in = (b_gate * inner_proj).astype(jnp.bfloat16).reshape(seq_count, seq_len, -1)
    padded = jnp.pad(gated_in, ((0, 0), (2, 0), (0, 0))).astype(jnp.float32)
    mask_one, mask_two = conv_masks(keep_mask)
    conv_out = conv_w[0] * padded[:, 2:] + conv_w[1] * padded[:, 1:-1] * mask_one + conv_w[2] * padded[:, :-2] * mask_two
    conv_out = conv_out.reshape(seq_count * seq_len, -1)
    mixed_out = (c_gate * conv_out).astype(jnp.bfloat16)
    after_mix = flat_rows + matmul(mixed_out, w_out.T)
    normed_two, inv_two = norm_forward(after_mix, gain_two)
    gate_pre = matmul(normed_two, w_gate)
    up_proj = matmul(normed_two, w_up)
    swish_out = (jax.nn.silu(gate_pre) * up_proj).astype(jnp.bfloat16)
    result = after_mix + matmul(swish_out, w_down.T)
    saved_acts = (flat_rows, normed_one, inv_one, b_gate, c_gate, inner_proj, padded, conv_out, mixed_out, after_mix, normed_two, inv_two, gate_pre, up_proj, swish_out)
    return (result.reshape(seq_count, seq_len, feature_dim), saved_acts)

def layer_backward(grad_out, keep_mask, params, saved_acts):
    gain_one, w_in, conv_w, w_out, gain_two, w_gate, w_up, w_down = params
    flat_rows, normed_one, inv_one, b_gate, c_gate, inner_proj, padded, conv_out, mixed_out, after_mix, normed_two, inv_two, gate_pre, up_proj, swish_out = saved_acts
    seq_count, seq_len, feature_dim = grad_out.shape
    grad_rows = grad_out.reshape(seq_count * seq_len, feature_dim)
    grad_low = grad_rows.astype(jnp.bfloat16)
    grad_swish = matmul(grad_low, w_down)
    grad_w_down = matmul(grad_low.T, swish_out)
    sigmoid_gate = jax.nn.sigmoid(gate_pre)
    grad_gate = (grad_swish * up_proj * sigmoid_gate * (1.0 + gate_pre * (1.0 - sigmoid_gate))).astype(jnp.bfloat16)
    grad_up = (grad_swish * gate_pre * sigmoid_gate).astype(jnp.bfloat16)
    grad_w_gate = matmul(normed_two.T, grad_gate)
    grad_w_up = matmul(normed_two.T, grad_up)
    grad_norm_two = matmul(grad_gate, w_gate.T) + matmul(grad_up, w_up.T)
    back_two, grad_gain_two = norm_backward(after_mix, inv_two, gain_two, grad_norm_two)
    grad_mix = grad_rows + back_two
    mix_low = grad_mix.astype(jnp.bfloat16)
    grad_mixed = matmul(mix_low, w_out)
    grad_w_out = matmul(mix_low.T, mixed_out)
    grad_c = (grad_mixed * conv_out).astype(jnp.bfloat16)
    grad_conv = (grad_mixed * c_gate).reshape(seq_count, seq_len, -1)
    mask_one, mask_two = conv_masks(keep_mask)
    grad_conv_w = jnp.stack([lax.optimization_barrier(jnp.sum(grad_conv * padded[:, 2:], axis=(0, 1))), lax.optimization_barrier(jnp.sum(grad_conv * mask_one * padded[:, 1:-1], axis=(0, 1))), lax.optimization_barrier(jnp.sum(grad_conv * mask_two * padded[:, :-2], axis=(0, 1)))])
    grad_padded = jnp.pad(conv_w[0] * grad_conv, ((0, 0), (2, 0), (0, 0))) + jnp.pad(conv_w[1] * grad_conv * mask_one, ((0, 0), (1, 1), (0, 0))) + jnp.pad(conv_w[2] * grad_conv * mask_two, ((0, 0), (0, 2), (0, 0)))
    grad_gated = grad_padded[:, 2:].reshape(seq_count * seq_len, -1)
    grad_b = (grad_gated * inner_proj).astype(jnp.bfloat16)
    grad_x = (grad_gated * b_gate).astype(jnp.bfloat16)
    grad_w_in = jnp.stack([matmul(normed_one.T, grad_b), matmul(normed_one.T, grad_c), matmul(normed_one.T, grad_x)])
    grad_norm_one = matmul(grad_b, w_in[0].T) + matmul(grad_c, w_in[1].T) + matmul(grad_x, w_in[2].T)
    back_one, grad_gain_one = norm_backward(flat_rows, inv_one, gain_one, grad_norm_one)
    grad_in = grad_mix + back_one
    weight_grads = (grad_gain_one, grad_w_in, grad_conv_w, grad_w_out, grad_gain_two, grad_w_gate, grad_w_up, grad_w_down)
    return (grad_in.reshape(seq_count, seq_len, feature_dim), weight_grads)

def reference(tokens, starts, cotangent, gain_one, w_in, conv_w, w_out, gain_two, w_gate, w_up, w_down):
    stacked = (gain_one, w_in, conv_w, w_out, gain_two, w_gate, w_up, w_down)
    layer_params = [tuple((weight[layer_index] for weight in stacked)) for layer_index in range(N_SECTION)]
    totals = [None for layer_index in range(N_SECTION)]
    outputs_list = []
    inputs_grads = []
    for mb_index in range(MICRO):
        keep_mask = 1.0 - starts[mb_index].astype(jnp.float32)
        hidden = tokens[mb_index].astype(jnp.float32)
        saved_all = []
        for layer_index in range(N_SECTION):
            if layer_index > 0:
                hidden = lax.optimization_barrier(hidden.astype(jnp.bfloat16)).astype(jnp.float32)
            hidden, saved_acts = layer_forward(hidden, keep_mask, layer_params[layer_index])
            saved_all.append(saved_acts)
        outputs_list.append(hidden)
        grad_hidden = cotangent[mb_index]
        for layer_index in reversed(range(N_SECTION)):
            grad_hidden, weight_grads = layer_backward(grad_hidden, keep_mask, layer_params[layer_index], saved_all[layer_index])
            if totals[layer_index] is None:
                totals[layer_index] = weight_grads
            else:
                totals[layer_index] = jax.tree.map(jnp.add, totals[layer_index], weight_grads)
        inputs_grads.append(grad_hidden)
    ends = jnp.stack([jnp.stack(inputs_grads), jnp.stack(outputs_list)])
    per_kind = [jnp.stack([totals[layer_index][kind_index] for layer_index in range(N_SECTION)]) for kind_index in range(8)]
    conv_grads = per_kind[2].reshape(N_SECTION, KW, N_MP, D // N_MP)
    return (ends, per_kind[0], per_kind[1], conv_grads, per_kind[3], per_kind[4], per_kind[5], per_kind[6], per_kind[7])
```

```python
import jax
import jax.numpy as jnp
from jax import lax
from jax.sharding import PartitionSpec as P

NORM_EPS = 1e-05
LOW = jnp.bfloat16
WIDE = jnp.float32


def shifted(x, axis, by):
    size = lax.axis_size(axis)
    pairs = [(i, i + by) for i in range(size) if 0 <= i + by < size]
    return lax.ppermute(x, axis, pairs)


def matmul(lhs_mat, rhs_mat):
    return jnp.dot(lhs_mat, rhs_mat, preferred_element_type=WIDE)


def matmul_rhs_t(lhs_mat, rhs_mat):
    return lax.dot_general(
        lhs_mat, rhs_mat, (((1,), (1,)), ((), ())), preferred_element_type=WIDE
    )


def matmul_lhs_t(lhs_mat, rhs_mat):
    return lax.dot_general(
        lhs_mat, rhs_mat, (((0,), (0,)), ((), ())), preferred_element_type=WIDE
    )


def swap_mp(x):
    return lax.ppermute(x, "mp", [(0, 1), (1, 0)])


def sum_mp(part):
    if lax.axis_size("mp") != 2:
        return lax.psum(part, "mp")
    low = part.astype(LOW)
    return low.astype(WIDE) + swap_mp(low).astype(WIDE)


def to_section(low, by):
    if lax.axis_size("mp") != 2:
        return shifted(low, "section", by)
    half = low.shape[0] // 2
    core = lax.axis_index("mp")
    mine = lax.dynamic_slice_in_dim(low, core * half, half, 0)
    mine = shifted(mine, "section", by)
    other = swap_mp(mine)
    first = jnp.where(core == 0, mine, other)
    second = jnp.where(core == 0, other, mine)
    return jnp.concatenate([first, second], axis=0)


def norm_forward(hidden, norm_gain):
    inv_rms = lax.rsqrt(jnp.mean(hidden * hidden, axis=-1, keepdims=True) + NORM_EPS)
    return (hidden * inv_rms * norm_gain).astype(LOW), inv_rms


def norm_backward(hidden, inv_rms, norm_gain, grad_norm, want_gain):
    normed = hidden * inv_rms
    scaled = grad_norm * norm_gain
    grad_gain = jnp.sum(grad_norm * normed, axis=0) if want_gain else None
    grad_hidden = inv_rms * (scaled - normed * jnp.mean(scaled * normed, axis=-1, keepdims=True))
    return grad_hidden, grad_gain


def layer_forward(hidden, masks, params, count, save):
    gain_one, w_in, conv_w, w_out, gain_two, w_gate, w_up, w_down = params
    mask_one, mask_two = masks
    rows = hidden.shape[0]
    normed_one, inv_one = norm_forward(hidden, gain_one)
    b_gate = matmul(normed_one, w_in[0])
    inner_proj = matmul(normed_one, w_in[2])
    gated_in = (b_gate * inner_proj).astype(LOW).reshape(count, rows // count, -1)
    recv_state = shifted(gated_in[:, -2:], "seq", 1)
    c_gate = matmul(normed_one, w_in[1])
    padded = jnp.concatenate([recv_state, gated_in], axis=1)
    conv_out = (
        conv_w[0] * padded[:, 2:].astype(WIDE)
        + conv_w[1] * padded[:, 1:-1].astype(WIDE) * mask_one
        + conv_w[2] * padded[:, :-2].astype(WIDE) * mask_two
    ).reshape(rows, -1)
    mixed_out = (c_gate * conv_out).astype(LOW)
    after_mix = hidden + sum_mp(matmul_rhs_t(mixed_out, w_out))
    normed_two, inv_two = norm_forward(after_mix, gain_two)
    gate_pre = matmul(normed_two, w_gate)
    up_proj = matmul(normed_two, w_up)
    sig = jax.nn.sigmoid(gate_pre)
    silu = gate_pre * sig
    swish_out = (silu * up_proj).astype(LOW)
    result = after_mix + sum_mp(matmul_rhs_t(swish_out, w_down))
    if not save:
        return result, None
    gate_slope = (up_proj * sig * (1.0 + gate_pre * (1.0 - sig))).astype(LOW)
    saved = (
        hidden, normed_one, inv_one, b_gate, c_gate, inner_proj, padded, conv_out, mixed_out,
        after_mix, normed_two, inv_two, gate_slope, silu.astype(LOW), swish_out,
    )
    return result, saved


def ring_order(lead, trail):
    order = []
    for first in range(lead):
        inner = range(trail) if first % 2 == 0 else reversed(range(trail))
        order += [first * trail + second for second in inner]
    return order


class Ring:
    def __init__(self):
        lead, trail = lax.axis_size("dp"), lax.axis_size("seq")
        self.size = lead * trail
        self.order = ring_order(lead, trail)
        dp_index, seq_index = lax.axis_index("dp"), lax.axis_index("seq")
        along = jnp.where(dp_index % 2 == 0, seq_index, trail - 1 - seq_index)
        place = dp_index * trail + along
        size = self.size
        order = jnp.array(self.order, jnp.int32)
        self.pieces = {
            way: [order[(place - way * (step + 1)) % size] for step in range(size)]
            for way in (1, -1)
        }

    def hop(self, value, way):
        size, order = self.size, self.order
        pairs = [(order[i], order[(i + way) % size]) for i in range(size)]
        return lax.ppermute(value, ("dp", "seq"), pairs)

    def own(self, parts, way, step):
        index = self.pieces[way][step]
        cut = []
        for part in parts:
            height = part.shape[0] // self.size
            cut.append(lax.dynamic_slice_in_dim(part, index * height, height, 0))
        return cut[0] if len(cut) == 1 else jnp.concatenate(cut, axis=1)


def add_low(one, two):
    return (one.astype(WIDE) + two.astype(WIDE)).astype(LOW)


def run_rings(ring, jobs):
    state = [ring.own(parts, way, 0) for parts, way in jobs]
    for step in range(1, ring.size):
        for slot, (parts, way) in enumerate(jobs):
            state[slot] = ring.hop(state[slot], way)
        for slot, (parts, way) in enumerate(jobs):
            state[slot] = add_low(ring.own(parts, way, step), state[slot])
    return state


def small_sum(vec):
    for axis in ("seq", "dp"):
        size = lax.axis_size(axis)
        if size & (size - 1):
            vec = lax.psum(vec, axis)
            continue
        bit = 1
        while bit < size:
            vec = vec + lax.ppermute(vec, axis, [(i, i ^ bit) for i in range(size)])
            bit *= 2
    return vec


def layer_backward(grad_rows, grad_low, masks, params, saved, count, ring):
    gain_one, w_in, conv_w, w_out, gain_two, w_gate, w_up, w_down = params
    (
        hidden, normed_one, inv_one, b_gate, c_gate, inner_proj, padded, conv_out, mixed_out,
        after_mix, normed_two, inv_two, gate_slope, silu, swish_out,
    ) = saved
    mask_one, mask_two = masks
    want = ring is not None
    rows = grad_rows.shape[0]
    grad_swish = matmul(grad_low, w_down)
    grad_gate = (grad_swish * gate_slope).astype(LOW)
    grad_up = (grad_swish * silu).astype(LOW)
    partial_two = matmul_rhs_t(grad_gate, w_gate) + matmul_rhs_t(grad_up, w_up)
    grad_norm_two = sum_mp(partial_two)
    back_two, grad_gain_two = norm_backward(after_mix, inv_two, gain_two, grad_norm_two, want)
    grad_mix = grad_rows + back_two
    mix_low = grad_mix.astype(LOW)
    grad_mixed = matmul(mix_low, w_out)
    grad_c = (grad_mixed * conv_out).astype(LOW)
    grad_conv = (grad_mixed * c_gate).reshape(count, rows // count, -1)
    masked_one = grad_conv * mask_one
    masked_two = grad_conv * mask_two
    edge = jnp.concatenate(
        [conv_w[2] * masked_two[:, :1], conv_w[2] * masked_two[:, 1:2] + conv_w[1] * masked_one[:, :1]],
        axis=1,
    )
    returned = shifted(edge, "seq", -1)
    one_next = jnp.concatenate([masked_one[:, 1:], jnp.zeros_like(masked_one[:, :1])], axis=1)
    two_next = jnp.concatenate([masked_two[:, 2:], jnp.zeros_like(masked_two[:, :2])], axis=1)
    grad_gated = conv_w[0] * grad_conv + conv_w[1] * one_next + conv_w[2] * two_next
    grad_gated = grad_gated.at[:, -2:].add(returned)
    grad_gated = grad_gated.reshape(rows, -1)
    grad_b = (grad_gated * inner_proj).astype(LOW)
    grad_x = (grad_gated * b_gate).astype(LOW)
    partial_one = (
        matmul_rhs_t(grad_c, w_in[1]) + matmul_rhs_t(grad_b, w_in[0]) + matmul_rhs_t(grad_x, w_in[2])
    )
    grad_norm_one = sum_mp(partial_one)
    back_one, grad_gain_one = norm_backward(hidden, inv_one, gain_one, grad_norm_one, want)
    grad_in = grad_mix + back_one
    if not want:
        return grad_in, None
    g_down = matmul_lhs_t(grad_low, swish_out).astype(LOW)
    g_gate = matmul_lhs_t(normed_two, grad_gate).astype(LOW)
    g_up = matmul_lhs_t(normed_two, grad_up).astype(LOW)
    g_out = matmul_lhs_t(mix_low, mixed_out).astype(LOW)
    g_in = [matmul_lhs_t(normed_one, part).astype(LOW) for part in (grad_b, grad_c, grad_x)]
    wide = padded.astype(WIDE)
    g_conv = jnp.stack(
        [
            jnp.sum(grad_conv * wide[:, 2:], axis=(0, 1)),
            jnp.sum(masked_one * wide[:, 1:-1], axis=(0, 1)),
            jnp.sum(masked_two * wide[:, :-2], axis=(0, 1)),
        ]
    )
    split = g_down.shape[1] // 256 * 128
    if split == 0:
        split = g_down.shape[1] // 2
    jobs = [
        ([g_down[:, :split]], 1),
        ([g_down[:, split:]], -1),
        ([g_gate], 1),
        ([g_up], -1),
        ([g_in[0], g_in[1]], 1),
        ([g_in[2], g_out], -1),
    ]
    down_a, down_b, o_gate, o_up, in_a, in_b = run_rings(ring, jobs)
    cut = g_in[0].shape[1]
    small = jnp.concatenate([grad_gain_one, grad_gain_two, g_conv.reshape(-1)])
    small = small_sum(small)
    width = grad_gain_one.shape[0]
    s_one, s_two, s_conv = small[:width], small[width : 2 * width], small[2 * width :].reshape(3, -1)
    group = lax.axis_index("dp") * lax.axis_size("seq") + lax.axis_index("seq")

    def piece(x):
        share = x.shape[-1] // ring.size
        return lax.dynamic_slice_in_dim(x, group * share, share, x.ndim - 1)

    grads = (
        piece(s_one),
        jnp.stack([in_a[:, :cut], in_a[:, cut:], in_b[:, :cut]]).astype(WIDE),
        piece(s_conv)[:, None, :],
        in_b[:, cut:].astype(WIDE),
        piece(s_two),
        o_gate.astype(WIDE),
        o_up.astype(WIDE),
        jnp.concatenate([down_a, down_b], axis=1).astype(WIDE),
    )
    return grad_in, grads


def on_device(
    tokens, starts, cotangent, gain_one, w_in, conv_w, w_out, gain_two, w_gate, w_up, w_down
):
    is_first = lax.axis_index("section") == 0
    shape = tokens.shape
    count, length, width = shape[0] * shape[1], shape[2], shape[3]
    params = (gain_one[0], w_in[0], conv_w[0], w_out[0], gain_two[0], w_gate[0], w_up[0], w_down[0])
    keep = 1.0 - starts.astype(WIDE).reshape(count, length)
    keep_before = shifted(keep[:, -1:], "seq", 1)
    before = jnp.concatenate([keep_before, keep[:, :-1]], axis=1)
    masks = lax.optimization_barrier((keep[:, :, None], (before * keep)[:, :, None]))
    tokens_rows = tokens.reshape(count * length, width)
    cot_rows = cotangent.reshape(count * length, width)

    result, _ = layer_forward(tokens_rows.astype(WIDE), masks, params, count, False)
    arriving = to_section(result.astype(LOW), 1)
    source = jnp.where(is_first, tokens_rows, arriving).astype(WIDE)
    result, saved = layer_forward(source, masks, params, count, True)
    grad_in, _ = layer_backward(cot_rows, cot_rows.astype(LOW), masks, params, saved, count, None)
    arriving = to_section(grad_in.astype(LOW), -1)
    grad_rows = jnp.where(is_first, arriving.astype(WIDE), cot_rows)
    grad_in, grads = layer_backward(
        grad_rows, grad_rows.astype(LOW), masks, params, saved, count, Ring()
    )
    ends = jnp.where(is_first, grad_in, result).reshape(shape)
    return (ends[None],) + tuple(part[None] for part in grads)


def solution(mesh):
    in_specs = (
        P(None, "dp", "seq", None),
        P(None, "dp", "seq"),
        P(None, "dp", "seq", None),
        P("section", None),
        P("section", None, None, "mp"),
        P("section", None, "mp"),
        P("section", None, "mp"),
        P("section", None),
        P("section", None, "mp"),
        P("section", None, "mp"),
        P("section", None, "mp"),
    )
    out_specs = (
        P("section", None, "dp", "seq", None),
        P("section", ("dp", "seq")),
        P("section", None, ("dp", "seq"), "mp"),
        P("section", None, "mp", ("dp", "seq")),
        P("section", ("dp", "seq"), "mp"),
        P("section", ("dp", "seq")),
        P("section", ("dp", "seq"), "mp"),
        P("section", ("dp", "seq"), "mp"),
        P("section", ("dp", "seq"), "mp"),
    )
    return jax.shard_map(
        on_device, mesh=mesh, in_specs=in_specs, out_specs=out_specs, check_vma=False
    )
```
